32 devices in a mesh: gx: 16 (over z, y, x), gy: 2 (over core).
Axes of the slice: x: 2, y: 2, z: 4, core: 2. Of those that a mesh axis runs over, the one named last changes fastest.
Arguments:
- right_side: float32 [64, 128, 128], P('gx', 'gy'), may hold values from -12 to 12
- phase: int32 [64, 128, 128], P('gx', 'gy'), may hold values from 0 to 1, as said below
Outputs:
- scaled_solution: float32 [64, 128, 128], P('gx', 'gy')
- residual: float32 [64, 128, 128], P('gx', 'gy')
The draws below stay inside these ranges and needn't reach their ends.
Inputs may be any that keep to these rules, and one draw needn't show every extreme that they name: `phase`: constant on each 2 x 2 x 2 block of cells that starts at even indices.
All inputs are finite; a program needn't handle non-finite values.
Results may differ from the reference program's by a relative error of at most 0.0024.
Values may be sent and summed in bfloat16 or wider, within the bound.
A program may use at most 64 MiB of HBM per device.

```python
import jax
import jax.numpy as jnp

NZ = 128
LEVELS = 6
NU = 2
COARSE_SWEEPS = 6
NX = 64
NY = 128


def draw_phase(key, part):
    blocks = jax.random.randint(jax.random.fold_in(key, 3), (NX // 2, NY // 2, NZ // 2), 0, 2, dtype=jnp.int32)
    return jnp.repeat(jnp.repeat(jnp.repeat(blocks, 2, 0), 2, 1), 2, 2)


def draw_right_side(key, part):
    noise = jax.random.normal(jax.random.fold_in(key, 11), (NX, NY, NZ), jnp.float32)
    values = noise
    return jnp.clip(values, -12.0, 12.0)


def setup_inputs(seed: int = 0) -> dict:
    splits = jax.random.split(jax.random.key(seed), 3)
    right_side = draw_right_side(jax.random.fold_in(splits[2], 71), 0)
    phase = draw_phase(jax.random.fold_in(splits[2], 71), 0)
    return dict(right_side=right_side, phase=phase)


OMEGA = 0.8


def harmonic(lower_cell, upper_cell):
    lower_value = jnp.where(lower_cell > 0, lower_cell, upper_cell)
    upper_value = jnp.where(upper_cell > 0, upper_cell, lower_cell)
    return (2.0 * lower_value * upper_value / (lower_value + upper_value)).astype(jnp.bfloat16)


def face_table(widened):
    face_x = harmonic(widened[:-1, 1:-1], widened[1:, 1:-1])
    face_y = harmonic(widened[1:-1, :-1], widened[1:-1, 1:])
    interior = jnp.pad(widened[1:-1, 1:-1], ((0, 0), (0, 0), (1, 1)), mode="edge")
    face_z = harmonic(interior[:, :, :-1], interior[:, :, 1:])
    return (face_x, face_y, face_z)


def pair_sum(values, dimension):
    dims_list = list(values.shape)
    dims_list[dimension:dimension + 1] = [dims_list[dimension] // 2, 2]
    return jnp.sum(values.reshape(dims_list), axis=dimension + 1)


def coarsen(faces):
    face_x, face_y, face_z = faces
    new_x = 0.25 * pair_sum(pair_sum(face_x.astype(jnp.float32)[0::2], 1), 2)
    new_y = 0.25 * pair_sum(pair_sum(face_y.astype(jnp.float32)[:, 0::2], 0), 2)
    new_z = 0.25 * pair_sum(pair_sum(face_z.astype(jnp.float32)[:, :, 0::2], 0), 1)
    return (new_x.astype(jnp.bfloat16), new_y.astype(jnp.bfloat16), new_z.astype(jnp.bfloat16))


def restrict(remainder):
    return 0.5 * pair_sum(pair_sum(pair_sum(remainder, 0), 1), 2)


def prolong(coarse):
    return jnp.repeat(jnp.repeat(jnp.repeat(coarse, 2, 0), 2, 1), 2, 2)


def centre_weight(faces):
    face_x, face_y, face_z = faces
    return (face_x[:-1].astype(jnp.float32) + face_x[1:].astype(jnp.float32)
            + face_y[:, :-1].astype(jnp.float32) + face_y[:, 1:].astype(jnp.float32)
            + face_z[:, :, :-1].astype(jnp.float32) + face_z[:, :, 1:].astype(jnp.float32))


def weighted(widened, faces):
    face_x, face_y, face_z = faces
    z_padded = jnp.pad(widened[1:-1, 1:-1], ((0, 0), (0, 0), (1, 1)))
    return (face_x[:-1] * widened[:-2, 1:-1] + face_x[1:] * widened[2:, 1:-1]
            + face_y[:, :-1] * widened[1:-1, :-2] + face_y[:, 1:] * widened[1:-1, 2:]
            + face_z[:, :, :-1] * z_padded[:, :, :-2] + face_z[:, :, 1:] * z_padded[:, :, 2:])


def cycle(source, faces, level_index):
    centre = centre_weight(faces)

    def operate(field):
        return centre * field - weighted(jnp.pad(field, ((1, 1), (1, 1), (0, 0))), faces)

    def smooth(field):
        return field + OMEGA * (source - operate(field)) / centre

    field = jnp.zeros_like(source)
    if level_index == LEVELS:
        for repeat in range(COARSE_SWEEPS):
            field = smooth(field)
        return field
    for repeat in range(NU):
        field = smooth(field)
    remainder = source - operate(field)
    coarse = cycle(restrict(remainder), coarsen(faces), level_index + 1)
    field = field + prolong(coarse)
    for repeat in range(NU):
        field = smooth(field)
    return field


def reference(right_side, phase):
    cell_beta = jnp.where(phase == 1, 1000.0, 1.0).astype(jnp.float32)
    widened = jnp.pad(cell_beta, ((1, 1), (1, 1), (0, 0)), mode="edge")
    faces = face_table(widened)
    solution = cycle(right_side, faces, 0)
    centre = centre_weight(faces)
    applied = centre * solution - weighted(jnp.pad(solution, ((1, 1), (1, 1), (0, 0))), faces)
    return centre * solution, right_side - applied
```

```python
import functools

import jax
import jax.numpy as jnp
import numpy as np
from jax import lax
from jax.experimental import pallas as pl
from jax.experimental.pallas import tpu as pltpu
from jax.sharding import PartitionSpec as P

LEVELS = 6
NU = 2
COARSE_SWEEPS = 6
OMEGA = 0.8
LIQUID, GAS = 1.0, 1000.0
MIXED = float(np.asarray(2.0 * LIQUID * GAS / (LIQUID + GAS), jnp.bfloat16))
MESH = pl.DeviceIdType.MESH
REACH = 3
EDGE = 8
EDGE_PHASE = 16
UNROLL = 16
LARGE = 1 << 20


def each(count, body):
    if count <= UNROLL:
        for i in range(count):
            body(i)
    else:
        lax.fori_loop(0, count, lambda i, carry: (body(i), carry)[1], 0)


def index_along(shape, axis):
    return lax.broadcasted_iota(jnp.int32, shape, axis)


def roll(x, shift, axis):
    return pltpu.roll(x, shift % x.shape[axis], axis)


def lane_bit(x, step):
    return index_along(x.shape, x.ndim - 1) // step % 2


def even_part(x, step):
    return jnp.where(lane_bit(x, step) == 0, x, roll(x, step, x.ndim - 1))


def odd_part(x, step):
    return jnp.where(lane_bit(x, step) == 1, x, roll(x, -step, x.ndim - 1))


def pair_lanes(x, step):
    axis = x.ndim - 1
    return x + jnp.where(lane_bit(x, step) == 0, roll(x, -step, axis), roll(x, step, axis))


def harmonic(a, b):
    low, high = jnp.minimum(a, b), jnp.maximum(a, b)
    return jnp.where((low == 0.0) | (low == high), high, MIXED)


def store(ref, i, value):
    ref[i] = value.astype(ref.dtype)


def wide(ref, i):
    return ref[i].astype(jnp.float32)


def quarter(x):
    return (0.25 * x).astype(jnp.bfloat16).astype(jnp.float32)


def kernel(ngx, ngy, counts, f_ref, phase_ref, scaled_ref, rest_ref, *refs):
    gx, gy = lax.axis_index("gx"), lax.axis_index("gy")
    n = ngx * ngy
    me = gx * ngy + gy
    lx, ly, nz = f_ref.shape
    by, cy = ly // 2, ly // 4
    refs = list(refs)

    def take(count):
        out = refs[:count]
        del refs[:count]
        return out

    (w0, wp, w1, gp, g2, p_pack, g1_pack, g2_pack, temp) = take(9)
    (b1, e2) = take(2)
    level_refs = [take(10) for _ in range(LEVELS + 1)]
    (s0, r0, s1, r1, sp, rp, sg, rg) = take(8)

    w0[...] = jnp.zeros(w0.shape, w0.dtype)
    wp[...] = jnp.zeros(wp.shape, wp.dtype)
    w1[...] = jnp.zeros(w1.shape, w1.dtype)

    barrier = pltpu.get_barrier_semaphore()

    def greet(k, carry):
        other = (me + k) % n
        pl.semaphore_signal(barrier, inc=1, device_id=(other // ngy, other % ngy), device_id_type=MESH)
        return carry

    lax.fori_loop(1, n, greet, 0)

    for plane in range(0, lx, 4):
        beta = [
            jnp.where(phase_ref[plane + 2 * k, pl.ds(0, by, 2), :] == 1, GAS, LIQUID) for k in range(2)
        ]
        p_pack[0] = jnp.where(lane_bit(beta[0], 1) == 0, beta[0], beta[1]).astype(jnp.bfloat16)
    for l in range(LEVELS + 1):
        for v in level_refs[l][:2]:
            zero = jnp.zeros(v.shape[1:], v.dtype)
            v[0] = zero
            v[v.shape[0] - 1] = zero

    pl.semaphore_wait(barrier, n - 1)

    def window_copy(src, dst, send, recv, reach, edge, d, e, slot, low_row):
        lead, rows = src.shape[0], src.shape[1]
        count = rows if e == 0 else edge
        source = src.at[:, pl.ds(rows - edge if e == 1 else 0, count), :]
        start = {0: edge, 1: 0, -1: edge + rows}[low_row]
        target = dst.at[pl.ds(slot * lead, lead), pl.ds(start, count), :]
        k = (d + reach) * 3 + e + 1
        return pltpu.make_async_remote_copy(
            src_ref=source, dst_ref=target, send_sem=send.at[k], recv_sem=recv.at[slot * 3 + 1 - low_row],
            device_id=(gx + d, gy + e), device_id_type=MESH,
        )

    def window(reach):
        for e in (0, 1, -1):
            for d in sorted(range(-reach, reach + 1), key=abs):
                if (d, e) != (0, 0):
                    there = (gx + d >= 0) & (gx + d < ngx) & (gy + e >= 0) & (gy + e < ngy)
                    yield d, e, there

    def window_send(src, dst, send, recv, reach, edge):
        for d, e, there in window(reach):
            @pl.when(there)
            def _():
                window_copy(src, dst, send, recv, reach, edge, d, e, reach - d, e).start()

    def window_wait(src, dst, send, recv, reach, edge):
        for d, e, there in window(reach):
            @pl.when(there)
            def _():
                window_copy(src, dst, send, recv, reach, edge, d, e, reach + d, -e).wait_recv()

    def window_done(src, dst, send, recv, reach, edge):
        for d, e, there in window(reach):
            @pl.when(there)
            def _():
                window_copy(src, dst, send, recv, reach, edge, d, e, reach - d, e).wait_send()

    def gather_send(src, dst, k):
        def body(t, carry):
            other = (me + t) % n
            pltpu.make_async_remote_copy(
                src_ref=src, dst_ref=dst.at[pl.ds(me, 1)], send_sem=sg.at[k], recv_sem=rg.at[k],
                device_id=(other // ngy, other % ngy), device_id_type=MESH,
            ).start()
            return carry

        lax.fori_loop(1, n, body, 0)

    def gather_all(dst, k):
        every = dst.at[pl.ds(0, n - 1)]
        return pltpu.make_async_remote_copy(
            src_ref=every, dst_ref=every, send_sem=sg.at[k], recv_sem=rg.at[k],
            device_id=(gx, (gy + 1) % ngy), device_id_type=MESH,
        )

    phase_window = (p_pack, wp, sp, rp, REACH, EDGE_PHASE)
    fine_window = (f_ref, w0, s0, r0, 1, EDGE)
    coarse_window = (g1_pack, w1, s1, r1, REACH, EDGE)
    window_send(*phase_window)
    window_send(*fine_window)
    gather_send(p_pack, gp, 0)

    wp[REACH, pl.ds(EDGE_PHASE, by), :] = p_pack[0]
    gp[me] = p_pack[0]
    w0[pl.ds(lx, lx), pl.ds(EDGE, ly), :] = f_ref[...]

    slots = temp.shape[0]

    def stretch(value, slot):
        rows = value.shape[0]
        temp[slot, pl.ds(0, rows, 2), :] = value
        temp[slot, pl.ds(1, rows, 2), :] = value

    def pair_rows(value, slot, first=True, second=True):
        rows = value.shape[0]
        temp[slot, pl.ds(0, rows), :] = value
        out = 0.0
        if first:
            out = out + temp[slot, pl.ds(0, rows // 2, 2), :]
        if second:
            out = out + temp[slot, pl.ds(1, rows // 2, 2), :]
        return out

    def neighbours(level, v_ref, i, step):
        (_, _, _, _, _, fx, fyl, fyh, fzl, fzh) = level
        v = v_ref[i + 1]
        return (
            wide(fx, i) * v_ref[i] + wide(fx, i + 1) * v_ref[i + 2]
            + wide(fyl, i) * roll(v, 1, 0) + wide(fyh, i) * roll(v, -1, 0)
            + wide(fzl, i) * roll(v, step, 1) + wide(fzh, i) * roll(v, -step, 1)
        )

    def sweep(level, source, target, step, first, last):
        f, inverse = level[2], level[3]

        def body(k):
            i = k + first
            target[i + 1] = (1.0 - OMEGA) * source[i + 1] + inverse[i] * (f[i] + neighbours(level, source, i, step))

        each(last - first, body)

    def rest_of(level, v_ref, i, step):
        return level[2][i] - level[4][i] * v_ref[i + 1] + neighbours(level, v_ref, i, step)

    def put_faces(level, i, inside, lows, step, edges):
        (_, _, _, inverse, centre, fx, fyl, fyh, fzl, fzh) = level
        (yl, yh, zl, zh) = lows
        total = wide(fx, i) + wide(fx, i + 1) + yl + yh + zl + zh
        inverse[i] = jnp.where(inside, OMEGA / jnp.where(inside, total, 1.0), 0.0)
        centre[i] = total
        lane = index_along(zl.shape, 1)
        fzl[i] = jnp.where(lane < step, 0.0, zl).astype(fzl.dtype)
        fzh[i] = jnp.where(lane >= nz - step, 0.0, zh).astype(fzh.dtype)
        if edges is not None:
            row = index_along(yl.shape, 0)
            yl = jnp.where(row == 0, 0.0, yl)
            yh = jnp.where(row >= edges - 1, 0.0, yh)
        fyl[i] = yl.astype(fyl.dtype)
        fyh[i] = yh.astype(fyh.dtype)

    def cell_faces(b, step):
        lane = index_along(b.shape, 1)
        yl, yh = harmonic(roll(b, 1, 0), b), harmonic(b, roll(b, -1, 0))
        zl = harmonic(jnp.where(lane < step, 0.0, roll(b, step, 1)), b)
        zh = harmonic(b, jnp.where(lane >= nz - step, 0.0, roll(b, -step, 1)))
        return yl, yh, zl, zh

    window_wait(*phase_window)
    for t in range(2 * REACH + 1):
        packed = wp[t].astype(jnp.float32)[EDGE_PHASE - EDGE : EDGE_PHASE + by + EDGE]
        b1[2 * t] = even_part(packed, 1)
        b1[2 * t + 1] = odd_part(packed, 1)

    level0 = level_refs[0]
    (va, vb, f0, inv0, c0, fx0) = level0[:6]
    rows0 = ly + 2 * EDGE
    blocks = 3 * lx // 2
    first_block = 2 * REACH - lx // 2
    before = None
    beta0 = []
    for j in range(-1, blocks + 1):
        stretch(b1[first_block + j], (j + 1) % slots)
        b = temp[(j + 1) % slots, pl.ds(EDGE, rows0), :]
        if before is not None:
            fx0[2 * j] = harmonic(before, b)
        if 0 <= j < blocks:
            fx0[2 * j + 1] = b
            beta0.append(b)
        before = b
    for j in range(blocks):
        lows = cell_faces(beta0[j], 1)
        for i in (2 * j, 2 * j + 1):
            put_faces(level0, i, beta0[j] > 0.0, lows, 1, None)

    window_wait(*fine_window)
    level0 = list(level0)
    level0[2] = w0
    planes0 = 3 * lx
    for i in range(planes0):
        va[i + 1] = inv0[i] * w0[i]
    sweep(level0, va, vb, 1, 1, planes0 - 1)
    rests = [rest_of(level0, vb, lx + i, 1)[EDGE : EDGE + ly] for i in range(lx)]
    coarse = [
        0.5 * pair_lanes(pair_rows(rests[2 * k] + rests[2 * k + 1], k % slots), 1) for k in range(lx // 2)
    ]
    packed = jnp.where(lane_bit(coarse[0], 1) == 0, coarse[0], coarse[1])
    g1_pack[0] = packed
    window_send(*coarse_window)
    w1[REACH, pl.ds(EDGE, by), :] = packed

    level1 = level_refs[1]
    (ua, ub, f1, inv1, c1, fx1) = level1[:6]
    planes1 = 2 * (2 * REACH + 1)
    fx1[0] = b1[0]
    fx1[planes1] = b1[planes1 - 1]
    for i in range(1, planes1):
        fx1[i] = harmonic(b1[i - 1], b1[i])
    for i in range(planes1):
        put_faces(level1, i, b1[i] > 0.0, cell_faces(b1[i], 2), 2, None)

    gather_all(gp, 0).wait_recv()

    def whole_plane(ref, k):
        parts = [ref[k * ngy + j].astype(jnp.float32) for j in range(ngy)]
        return jnp.concatenate(parts, axis=0)

    shape2 = counts[2]
    (nx2, ny2) = shape2
    level2 = level_refs[2]
    row1 = index_along((2 * ny2, nz), 0)

    raw = {}
    for l in range(2, LEVELS + 1):
        raw[l] = level_refs[l][6:10]

    def faces2(i):
        pack = whole_plane(gp, i)
        b = [even_part(pack, 1), odd_part(pack, 1)]
        if isinstance(i, int):
            below = odd_part(whole_plane(gp, i - 1), 1) if i > 0 else jnp.zeros_like(b[0])
        else:
            below = jnp.where(i > 0, odd_part(whole_plane(gp, jnp.maximum(i - 1, 0)), 1), 0.0)
        slot = 4 * (i % 2)
        store(level2[5], i, quarter(pair_lanes(pair_rows(harmonic(below, b[0]), slot), 2)))
        last = row1 == 2 * ny2 - 1
        yl = sum(harmonic(jnp.where(row1 == 0, 0.0, roll(x, 1, 0)), x) for x in b)
        yh = sum(harmonic(x, jnp.where(last, 0.0, roll(x, -1, 0))) for x in b)
        lane = index_along(b[0].shape, 1)
        zl = sum(harmonic(jnp.where(lane < 2, 0.0, roll(x, 2, 1)), x) for x in b)
        zh = sum(harmonic(x, jnp.where(lane >= nz - 2, 0.0, roll(x, -2, 1))) for x in b)
        store(raw[2][0], i, quarter(pair_lanes(pair_rows(yl, slot + 1, second=False), 2)))
        store(raw[2][1], i, quarter(pair_lanes(pair_rows(yh, slot + 2, first=False), 2)))
        store(raw[2][2], i, quarter(even_part(pair_rows(zl, slot + 3), 2)))
        store(raw[2][3], i, quarter(odd_part(pair_rows(zh, slot), 2)))

    each(nx2, faces2)
    top = odd_part(whole_plane(gp, nx2 - 1), 1)
    store(level2[5], nx2, quarter(pair_lanes(pair_rows(top, 5), 2)))

    for l in range(2, LEVELS + 1):
        nx, ny = counts[l]
        step = 2**l
        level = level_refs[l]
        if l < LEVELS:
            finer, coarser = level_refs[l], level_refs[l + 1]
            size = max(ny // 2, 4)
            if ny // 2 < EDGE:
                for ref in coarser[5:10]:
                    ref[...] = jnp.zeros(ref.shape, ref.dtype)

            def put(ref, i, value):
                ref[i, pl.ds(0, size), :] = quarter(value).astype(ref.dtype)

            def coarsen(i):
                slot = 4 * (i % 2)
                (fx, yl, yh, zl, zh) = finer[5:10]
                a, b = 2 * i, 2 * i + 1
                put(coarser[5], i, pair_lanes(pair_rows(wide(fx, a), slot), step))
                put(coarser[6], i, pair_lanes(pair_rows(wide(yl, a) + wide(yl, b), slot + 1, second=False), step))
                put(coarser[7], i, pair_lanes(pair_rows(wide(yh, a) + wide(yh, b), slot + 2, first=False), step))
                put(coarser[8], i, even_part(pair_rows(wide(zl, a) + wide(zl, b), slot + 3), step))
                put(coarser[9], i, odd_part(pair_rows(wide(zh, a) + wide(zh, b), slot), step))

            each(nx // 2, coarsen)
            put(coarser[5], nx // 2, pair_lanes(pair_rows(wide(finer[5], nx), 5), step))

        def finish(i):
            lows = [wide(ref, i) for ref in level[6:10]]
            inside = index_along(lows[0].shape, 0) < ny
            put_faces(level, i, inside, lows, step, ny)

        each(nx, finish)

    window_wait(*coarse_window)
    for t in range(2 * REACH + 1):
        f1[2 * t] = even_part(w1[t], 1)
        f1[2 * t + 1] = odd_part(w1[t], 1)
    for i in range(planes1):
        ua[i + 1] = inv1[i] * f1[i]
    sweep(level1, ua, ub, 2, 1, planes1 - 1)
    rests = [rest_of(level1, ub, 2 * REACH + i, 2)[EDGE : EDGE + by] for i in range(2)]
    coarse = 0.5 * pair_lanes(pair_rows(rests[0] + rests[1], 0), 2)
    half = cy // 2
    packed = jnp.where(lane_bit(coarse[:half], 1) == 0, coarse[:half], coarse[half:])
    g2_pack[0] = packed
    gather_send(g2_pack, g2, 1)
    g2[me] = packed
    gather_all(g2, 1).wait_recv()

    f2 = level2[2]

    def unpack(i):
        parts = []
        for j in range(ngy):
            pack = g2[i * ngy + j]
            parts += [even_part(pack, 1), odd_part(pack, 1)]
        f2[i] = jnp.concatenate(parts, axis=0)

    each(nx2, unpack)

    def cycle(l):
        nx, ny = counts[l]
        step = 2**l
        level = level_refs[l]
        (xa, xb, f, inverse) = level[:4]

        def begin(i):
            xa[i + 1] = inverse[i] * f[i]

        each(nx, begin)
        if l == LEVELS:
            for repeat in range(COARSE_SWEEPS - 1):
                sweep(level, xa, xb, step, 0, nx)
                xa, xb = xb, xa
            return xa
        for repeat in range(NU - 1):
            sweep(level, xa, xb, step, 0, nx)
            xa, xb = xb, xa
        f_next = level_refs[l + 1][2]
        size = max(ny // 2, 4)
        if ny // 2 < EDGE:
            f_next[...] = jnp.zeros(f_next.shape, f_next.dtype)

        def restrict(i):
            r = rest_of(level, xa, 2 * i, step) + rest_of(level, xa, 2 * i + 1, step)
            f_next[i, pl.ds(0, size), :] = 0.5 * pair_lanes(pair_rows(r, i % slots), step)

        each(nx // 2, restrict)
        fine = cycle(l + 1)

        def correct(i):
            slot = i % slots
            stretch(fine[i + 1], slot)
            e = temp[slot, pl.ds(0, xa.shape[1]), :]
            xb[2 * i + 1] = xa[2 * i + 1] + e
            xb[2 * i + 2] = xa[2 * i + 2] + e

        each(nx // 2, correct)
        xa, xb = xb, xa
        for repeat in range(NU):
            sweep(level, xa, xb, step, 0, nx)
            xa, xb = xb, xa
        return xa

    found = cycle(2)

    row2 = pl.multiple_of(gy * cy, 8)
    below2 = pl.multiple_of(jnp.maximum(gy * cy - EDGE, 0), 8)
    above2 = pl.multiple_of(jnp.minimum(gy * cy + cy, ny2 - EDGE), 8)
    for t in range(2 * REACH + 1):
        x = gx + t - REACH
        there = (x >= 0) & (x < nx2)
        plane = jnp.clip(x, 0, nx2 - 1) + 1
        e2[t, pl.ds(EDGE, cy), :] = jnp.where(there, found[plane, pl.ds(row2, cy), :], 0.0)
        low = found[plane, pl.ds(below2, EDGE), :]
        high = found[plane, pl.ds(above2, EDGE), :]
        e2[t, pl.ds(0, EDGE), :] = jnp.where(there & (gy > 0), low, 0.0)
        e2[t, pl.ds(EDGE + cy, EDGE), :] = jnp.where(there & (gy < ngy - 1), high, 0.0)

    for t in range(2 * REACH + 1):
        slot = t % slots
        stretch(e2[t], slot)
        e = temp[slot, pl.ds(EDGE, by + 2 * EDGE), :]
        ua[2 * t + 1] = ub[2 * t + 1] + e
        ua[2 * t + 2] = ub[2 * t + 2] + e
    sweep(level1, ua, ub, 2, 2, planes1 - 2)
    sweep(level1, ub, ua, 2, 3, planes1 - 3)

    for j in range(blocks):
        slot = j % slots
        stretch(ua[first_block + j + 1], slot)
        e = temp[slot, pl.ds(EDGE, rows0), :]
        va[2 * j + 1] = vb[2 * j + 1] + e
        va[2 * j + 2] = vb[2 * j + 2] + e
    sweep(level0, va, vb, 1, 2, planes0 - 2)
    sweep(level0, vb, va, 1, 3, planes0 - 3)
    for i in range(lx):
        product = c0[lx + i] * va[lx + i + 1]
        near = neighbours(level0, va, lx + i, 1)
        own = slice(EDGE, EDGE + ly)
        scaled_ref[i] = product[own]
        rest_ref[i] = w0[lx + i, pl.ds(EDGE, ly), :] - product[own] + near[own]

    window_done(*phase_window)
    window_done(*fine_window)
    window_done(*coarse_window)
    gather_all(gp, 0).wait_send()
    gather_all(g2, 1).wait_send()


def solution(mesh):
    ngx, ngy = mesh.shape["gx"], mesh.shape["gy"]
    n = ngx * ngy

    def on_device(right_side, phase):
        lx, ly, nz = right_side.shape
        assert lx == 4 and ly % 32 == 0 and NU == 2
        by, cy = ly // 2, ly // 4
        counts = [(lx * ngx >> l, ly * ngy >> l) for l in range(LEVELS + 1)]
        blocks = 2 * REACH + 1

        def level_scratch(planes, rows, padded_source=False):
            shapes = [planes + 2, planes + 2, planes, planes, planes, planes + 1] + [planes] * 4
            if padded_source:
                shapes[2] = 1
            large = planes * rows * nz * 4 >= LARGE
            types = [jnp.float32] * 5 + [jnp.bfloat16 if large else jnp.float32] * 5
            return [pltpu.VMEM((k, rows, nz), dtype) for k, dtype in zip(shapes, types)]

        scratch = [
            pltpu.VMEM((3 * lx, ly + 2 * EDGE, nz), jnp.float32),
            pltpu.VMEM((blocks, by + 2 * EDGE_PHASE, nz), jnp.bfloat16),
            pltpu.VMEM((blocks, by + 2 * EDGE, nz), jnp.float32),
            pltpu.VMEM((n, by, nz), jnp.bfloat16),
            pltpu.VMEM((n, cy // 2, nz), jnp.float32),
            pltpu.VMEM((1, by, nz), jnp.bfloat16),
            pltpu.VMEM((1, by, nz), jnp.float32),
            pltpu.VMEM((1, cy // 2, nz), jnp.float32),
            pltpu.VMEM((8, max(2 * (by + 2 * EDGE), 2 * counts[2][1], 2 * (cy + 2 * EDGE)), nz), jnp.float32),
            pltpu.VMEM((2 * blocks, by + 2 * EDGE, nz), jnp.float32),
            pltpu.VMEM((blocks, cy + 2 * EDGE, nz), jnp.float32),
        ]
        scratch += level_scratch(3 * lx, ly + 2 * EDGE, True)
        scratch += level_scratch(2 * blocks, by + 2 * EDGE)
        for l in range(2, LEVELS + 1):
            scratch += level_scratch(counts[l][0], max(counts[l][1], EDGE))
        scratch += [pltpu.SemaphoreType.DMA((9,))] * 2
        scratch += [pltpu.SemaphoreType.DMA((3 * blocks,))] * 4
        scratch += [pltpu.SemaphoreType.DMA((2,))] * 2
        return pl.pallas_call(
            functools.partial(kernel, ngx, ngy, counts),
            out_shape=[jax.ShapeDtypeStruct(right_side.shape, jnp.float32)] * 2,
            in_specs=[pl.BlockSpec(memory_space=pltpu.VMEM)] * 2,
            out_specs=[pl.BlockSpec(memory_space=pltpu.VMEM)] * 2,
            scratch_shapes=scratch,
            compiler_params=pltpu.CompilerParams(
                collective_id=0, has_side_effects=True, vmem_limit_bytes=66_000_000
            ),
        )(right_side, phase)

    placed = P("gx", "gy", None)
    return jax.shard_map(
        on_device, mesh=mesh, in_specs=(placed, placed), out_specs=(placed, placed), check_vma=False
    )
```

```python
import functools

import jax
import jax.numpy as jnp
import numpy as np
from jax import lax
from jax.experimental import pallas as pl
from jax.experimental.pallas import tpu as pltpu
from jax.sharding import PartitionSpec as P

LEVELS = 6
NU = 2
COARSE_SWEEPS = 6
OMEGA = 0.8
LIQUID, GAS = 1.0, 1000.0
MIXED = float(np.asarray(2.0 * LIQUID * GAS / (LIQUID + GAS), jnp.bfloat16))
MESH = pl.DeviceIdType.MESH
REACH = 3
EDGE = 8
EDGE_PHASE = 16
UNROLL = 16
LARGE = 1 << 20


def each(count, body):
    if count <= UNROLL:
        for i in range(count):
            body(i)
    else:
        lax.fori_loop(0, count, lambda i, carry: (body(i), carry)[1], 0)


def index_along(shape, axis):
    return lax.broadcasted_iota(jnp.int32, shape, axis)


def roll(x, shift, axis):
    return pltpu.roll(x, shift % x.shape[axis], axis)


def lane_bit(x, step):
    return index_along(x.shape, x.ndim - 1) // step % 2


def even_part(x, step):
    return jnp.where(lane_bit(x, step) == 0, x, roll(x, step, x.ndim - 1))


def odd_part(x, step):
    return jnp.where(lane_bit(x, step) == 1, x, roll(x, -step, x.ndim - 1))


def pair_lanes(x, step):
    axis = x.ndim - 1
    return x + jnp.where(lane_bit(x, step) == 0, roll(x, -step, axis), roll(x, step, axis))


def harmonic(a, b):
    low, high = jnp.minimum(a, b), jnp.maximum(a, b)
    return jnp.where((low == 0.0) | (low == high), high, MIXED)


def store(ref, i, value):
    ref[i] = value.astype(ref.dtype)


def wide(ref, i):
    return ref[i].astype(jnp.float32)


def quarter(x):
    return (0.25 * x).astype(jnp.bfloat16).astype(jnp.float32)


def kernel(ngx, ngy, counts, f_ref, phase_ref, scaled_ref, rest_ref, *refs):
    gx, gy = lax.axis_index("gx"), lax.axis_index("gy")
    n = ngx * ngy
    me = gx * ngy + gy
    lx, ly, nz = f_ref.shape
    by, cy = ly // 2, ly // 4
    refs = list(refs)

    def take(count):
        out = refs[:count]
        del refs[:count]
        return out

    (w0, wp, w1, gp, g2, p_pack, g1_pack, g2_pack, temp) = take(9)
    (b1, e2) = take(2)
    level_refs = [take(10) for _ in range(LEVELS + 1)]
    (s0, r0, sf, rf, s1, r1, sp, rp, sg, rg) = take(10)

    w0[...] = jnp.zeros(w0.shape, w0.dtype)
    wp[...] = jnp.zeros(wp.shape, wp.dtype)
    w1[...] = jnp.zeros(w1.shape, w1.dtype)

    barrier = pltpu.get_barrier_semaphore()

    def greet(k, carry):
        other = (me + k) % n
        pl.semaphore_signal(barrier, inc=1, device_id=(other // ngy, other % ngy), device_id_type=MESH)
        return carry

    lax.fori_loop(1, n, greet, 0)

    for plane in range(0, lx, 4):
        beta = [
            jnp.where(phase_ref[plane + 2 * k, pl.ds(0, by, 2), :] == 1, GAS, LIQUID) for k in range(2)
        ]
        p_pack[0] = jnp.where(lane_bit(beta[0], 1) == 0, beta[0], beta[1]).astype(jnp.bfloat16)
    for l in range(LEVELS + 1):
        for v in level_refs[l][:2]:
            zero = jnp.zeros(v.shape[1:], v.dtype)
            v[0] = zero
            v[v.shape[0] - 1] = zero

    pl.semaphore_wait(barrier, n - 1)

    def window_copy(src, dst, send, recv, reach, edge, half, d, e, slot, low_row, toward):
        lead, rows = src.shape[0], src.shape[1]
        plane, planes = 0, lead
        if half is not None and d != 0:
            planes = lead // 2
            plane = planes if (toward > 0) == (half == 0) else 0
        count = rows if e == 0 else edge
        source = src.at[pl.ds(plane, planes), pl.ds(rows - edge if e == 1 else 0, count), :]
        start = {0: edge, 1: 0, -1: edge + rows}[low_row]
        target = dst.at[pl.ds(slot * lead + plane, planes), pl.ds(start, count), :]
        k = (d + reach) * 3 + e + 1
        return pltpu.make_async_remote_copy(
            src_ref=source, dst_ref=target, send_sem=send.at[k], recv_sem=recv.at[slot * 3 + 1 - low_row],
            device_id=(gx + d, gy + e), device_id_type=MESH,
        )

    def window(low, high):
        for e in (0, 1, -1):
            for d in sorted(range(-high, high + 1), key=abs):
                if (d, e) != (0, 0) and abs(d) >= low:
                    there = (gx + d >= 0) & (gx + d < ngx) & (gy + e >= 0) & (gy + e < ngy)
                    yield d, e, there

    def window_send(refs, low, high, half=None):
        reach = refs[4]
        for d, e, there in window(low, high):
            @pl.when(there)
            def _():
                window_copy(*refs, half, d, e, reach - d, e, d).start()

    def window_wait(refs, low, high, half=None):
        reach = refs[4]
        for d, e, there in window(low, high):
            @pl.when(there)
            def _():
                window_copy(*refs, half, d, e, reach + d, -e, -d).wait_recv()

    def window_done(refs, low, high, half=None):
        reach = refs[4]
        for d, e, there in window(low, high):
            @pl.when(there)
            def _():
                window_copy(*refs, half, d, e, reach - d, e, d).wait_send()

    def gather_send(src, dst, k):
        def body(t, carry):
            other = (me + t) % n
            pltpu.make_async_remote_copy(
                src_ref=src, dst_ref=dst.at[pl.ds(me, 1)], send_sem=sg.at[k], recv_sem=rg.at[k],
                device_id=(other // ngy, other % ngy), device_id_type=MESH,
            ).start()
            return carry

        lax.fori_loop(1, n, body, 0)

    def gather_all(dst, k):
        every = dst.at[pl.ds(0, n - 1)]
        return pltpu.make_async_remote_copy(
            src_ref=every, dst_ref=every, send_sem=sg.at[k], recv_sem=rg.at[k],
            device_id=(gx, (gy + 1) % ngy), device_id_type=MESH,
        )

    phase_window = (p_pack, wp, sp, rp, REACH, EDGE_PHASE)
    near_window = (f_ref, w0, s0, r0, 1, EDGE)
    far_window = (f_ref, w0, sf, rf, 1, EDGE)
    coarse_window = (g1_pack, w1, s1, r1, REACH, EDGE)
    window_send(phase_window, 0, 1)
    window_send(near_window, 0, 1, 0)
    window_send(phase_window, 2, REACH)

    wp[REACH, pl.ds(EDGE_PHASE, by), :] = p_pack[0]
    gp[me] = p_pack[0]
    w0[pl.ds(lx, lx), pl.ds(EDGE, ly), :] = f_ref[...]

    slots = temp.shape[0]

    def stretch(value, slot):
        rows = value.shape[0]
        temp[slot, pl.ds(0, rows, 2), :] = value
        temp[slot, pl.ds(1, rows, 2), :] = value

    def pair_rows(value, slot, first=True, second=True):
        rows = value.shape[0]
        temp[slot, pl.ds(0, rows), :] = value
        out = 0.0
        if first:
            out = out + temp[slot, pl.ds(0, rows // 2, 2), :]
        if second:
            out = out + temp[slot, pl.ds(1, rows // 2, 2), :]
        return out

    def neighbours(level, v_ref, i, step):
        (_, _, _, _, _, fx, fyl, fyh, fzl, fzh) = level
        v = v_ref[i + 1]
        return (
            wide(fx, i) * v_ref[i] + wide(fx, i + 1) * v_ref[i + 2]
            + wide(fyl, i) * roll(v, 1, 0) + wide(fyh, i) * roll(v, -1, 0)
            + wide(fzl, i) * roll(v, step, 1) + wide(fzh, i) * roll(v, -step, 1)
        )

    def sweep(level, source, target, step, first, last):
        f, inverse = level[2], level[3]

        def body(k):
            i = k + first
            target[i + 1] = (1.0 - OMEGA) * source[i + 1] + inverse[i] * (f[i] + neighbours(level, source, i, step))

        each(last - first, body)

    def rest_of(level, v_ref, i, step):
        return level[2][i] - level[4][i] * v_ref[i + 1] + neighbours(level, v_ref, i, step)

    def put_faces(level, i, inside, lows, step, edges):
        (_, _, _, inverse, centre, fx, fyl, fyh, fzl, fzh) = level
        (yl, yh, zl, zh) = lows
        total = wide(fx, i) + wide(fx, i + 1) + yl + yh + zl + zh
        inverse[i] = jnp.where(inside, OMEGA / jnp.where(inside, total, 1.0), 0.0)
        centre[i] = total
        lane = index_along(zl.shape, 1)
        fzl[i] = jnp.where(lane < step, 0.0, zl).astype(fzl.dtype)
        fzh[i] = jnp.where(lane >= nz - step, 0.0, zh).astype(fzh.dtype)
        if edges is not None:
            row = index_along(yl.shape, 0)
            yl = jnp.where(row == 0, 0.0, yl)
            yh = jnp.where(row >= edges - 1, 0.0, yh)
        fyl[i] = yl.astype(fyl.dtype)
        fyh[i] = yh.astype(fyh.dtype)

    def cell_faces(b, step):
        lane = index_along(b.shape, 1)
        yl, yh = harmonic(roll(b, 1, 0), b), harmonic(b, roll(b, -1, 0))
        zl = harmonic(jnp.where(lane < step, 0.0, roll(b, step, 1)), b)
        zh = harmonic(b, jnp.where(lane >= nz - step, 0.0, roll(b, -step, 1)))
        return yl, yh, zl, zh

    def phase_block(t):
        packed = wp[t].astype(jnp.float32)[EDGE_PHASE - EDGE : EDGE_PHASE + by + EDGE]
        b1[2 * t] = even_part(packed, 1)
        b1[2 * t + 1] = odd_part(packed, 1)

    window_wait(phase_window, 0, 1)
    for t in range(REACH - 1, REACH + 2):
        phase_block(t)

    level0 = list(level_refs[0])
    level0[2] = w0
    (va, vb, f0, inv0, c0, fx0) = level0[:6]
    rows0 = ly + 2 * EDGE
    blocks = 3 * lx // 2
    first_block = 2 * REACH - lx // 2
    planes0 = 3 * lx
    near0, near1 = lx - 2, 2 * lx + 2

    def fine_beta(j):
        slot = (j + 1) % slots
        stretch(b1[first_block + j], slot)
        return temp[slot, pl.ds(EDGE, rows0), :]

    def fine_faces(j):
        lows = cell_faces(beta0[j], 1)
        for i in (2 * j, 2 * j + 1):
            put_faces(level0, i, beta0[j] > 0.0, lows, 1, None)

    beta0 = [fine_beta(j) for j in range(blocks)]
    for j in range(blocks):
        if j > 0:
            fx0[2 * j] = harmonic(beta0[j - 1], beta0[j])
        fx0[2 * j + 1] = beta0[j]
    for j in range(near0 // 2, near1 // 2):
        fine_faces(j)

    window_wait(near_window, 0, 1, 0)
    window_send(far_window, 1, 1, 1)
    gather_send(p_pack, gp, 0)
    for i in range(near0, near1):
        va[i + 1] = inv0[i] * w0[i]
    sweep(level0, va, vb, 1, near0 + 1, near1 - 1)
    rests = [rest_of(level0, vb, lx + i, 1)[EDGE : EDGE + ly] for i in range(lx)]
    coarse = [
        0.5 * pair_lanes(pair_rows(rests[2 * k] + rests[2 * k + 1], k % slots), 1) for k in range(lx // 2)
    ]
    packed = jnp.where(lane_bit(coarse[0], 1) == 0, coarse[0], coarse[1])
    g1_pack[0] = packed
    window_send(coarse_window, 0, 1)
    window_send(coarse_window, 2, REACH)
    w1[REACH, pl.ds(EDGE, by), :] = packed

    window_wait(phase_window, 2, REACH)
    for t in range(2 * REACH + 1):
        if abs(t - REACH) > 1:
            phase_block(t)
    level1 = level_refs[1]
    (ua, ub, f1, inv1, c1, fx1) = level1[:6]
    planes1 = 2 * (2 * REACH + 1)
    fx1[0] = b1[0]
    fx1[planes1] = b1[planes1 - 1]
    for i in range(1, planes1):
        fx1[i] = harmonic(b1[i - 1], b1[i])
    for i in range(planes1):
        put_faces(level1, i, b1[i] > 0.0, cell_faces(b1[i], 2), 2, None)

    gather_all(gp, 0).wait_recv()

    def whole_plane(ref, k):
        parts = [ref[k * ngy + j].astype(jnp.float32) for j in range(ngy)]
        return jnp.concatenate(parts, axis=0)

    shape2 = counts[2]
    (nx2, ny2) = shape2
    level2 = level_refs[2]
    row1 = index_along((2 * ny2, nz), 0)

    raw = {}
    for l in range(2, LEVELS + 1):
        raw[l] = level_refs[l][6:10]

    def faces2(i):
        pack = whole_plane(gp, i)
        b = [even_part(pack, 1), odd_part(pack, 1)]
        if isinstance(i, int):
            below = odd_part(whole_plane(gp, i - 1), 1) if i > 0 else jnp.zeros_like(b[0])
        else:
            below = jnp.where(i > 0, odd_part(whole_plane(gp, jnp.maximum(i - 1, 0)), 1), 0.0)
        slot = 4 * (i % 2)
        store(level2[5], i, quarter(pair_lanes(pair_rows(harmonic(below, b[0]), slot), 2)))
        last = row1 == 2 * ny2 - 1
        yl = sum(harmonic(jnp.where(row1 == 0, 0.0, roll(x, 1, 0)), x) for x in b)
        yh = sum(harmonic(x, jnp.where(last, 0.0, roll(x, -1, 0))) for x in b)
        lane = index_along(b[0].shape, 1)
        zl = sum(harmonic(jnp.where(lane < 2, 0.0, roll(x, 2, 1)), x) for x in b)
        zh = sum(harmonic(x, jnp.where(lane >= nz - 2, 0.0, roll(x, -2, 1))) for x in b)
        store(raw[2][0], i, quarter(pair_lanes(pair_rows(yl, slot + 1, second=False), 2)))
        store(raw[2][1], i, quarter(pair_lanes(pair_rows(yh, slot + 2, first=False), 2)))
        store(raw[2][2], i, quarter(even_part(pair_rows(zl, slot + 3), 2)))
        store(raw[2][3], i, quarter(odd_part(pair_rows(zh, slot), 2)))

    each(nx2, faces2)
    top = odd_part(whole_plane(gp, nx2 - 1), 1)
    store(level2[5], nx2, quarter(pair_lanes(pair_rows(top, 5), 2)))

    for l in range(2, LEVELS + 1):
        nx, ny = counts[l]
        step = 2**l
        level = level_refs[l]
        if l < LEVELS:
            finer, coarser = level_refs[l], level_refs[l + 1]
            size = max(ny // 2, 4)
            if ny // 2 < EDGE:
                for ref in coarser[5:10]:
                    ref[...] = jnp.zeros(ref.shape, ref.dtype)

            def put(ref, i, value):
                ref[i, pl.ds(0, size), :] = quarter(value).astype(ref.dtype)

            def coarsen(i):
                slot = 4 * (i % 2)
                (fx, yl, yh, zl, zh) = finer[5:10]
                a, b = 2 * i, 2 * i + 1
                put(coarser[5], i, pair_lanes(pair_rows(wide(fx, a), slot), step))
                put(coarser[6], i, pair_lanes(pair_rows(wide(yl, a) + wide(yl, b), slot + 1, second=False), step))
                put(coarser[7], i, pair_lanes(pair_rows(wide(yh, a) + wide(yh, b), slot + 2, first=False), step))
                put(coarser[8], i, even_part(pair_rows(wide(zl, a) + wide(zl, b), slot + 3), step))
                put(coarser[9], i, odd_part(pair_rows(wide(zh, a) + wide(zh, b), slot), step))

            each(nx // 2, coarsen)
            put(coarser[5], nx // 2, pair_lanes(pair_rows(wide(finer[5], nx), 5), step))

        def finish(i):
            lows = [wide(ref, i) for ref in level[6:10]]
            inside = index_along(lows[0].shape, 0) < ny
            put_faces(level, i, inside, lows, step, ny)

        each(nx, finish)

    def coarse_block(t):
        f1[2 * t] = even_part(w1[t], 1)
        f1[2 * t + 1] = odd_part(w1[t], 1)
        for i in (2 * t, 2 * t + 1):
            ua[i + 1] = inv1[i] * f1[i]

    own1 = 2 * REACH
    window_wait(coarse_window, 0, 1)
    for t in range(REACH - 1, REACH + 2):
        coarse_block(t)
    sweep(level1, ua, ub, 2, own1 - 1, own1 + 3)
    rests = [rest_of(level1, ub, own1 + i, 2)[EDGE : EDGE + by] for i in range(2)]
    coarse = 0.5 * pair_lanes(pair_rows(rests[0] + rests[1], 0), 2)
    half = cy // 2
    packed = jnp.where(lane_bit(coarse[:half], 1) == 0, coarse[:half], coarse[half:])
    g2_pack[0] = packed
    gather_send(g2_pack, g2, 1)
    g2[me] = packed

    window_wait(coarse_window, 2, REACH)
    for t in range(2 * REACH + 1):
        if abs(t - REACH) > 1:
            coarse_block(t)
    sweep(level1, ua, ub, 2, 1, own1 - 1)
    sweep(level1, ua, ub, 2, own1 + 3, planes1 - 1)

    fx0[0] = harmonic(fine_beta(-1), beta0[0])
    fx0[planes0] = harmonic(beta0[blocks - 1], fine_beta(blocks))
    window_wait(far_window, 1, 1, 1)
    for j in range(blocks):
        if not near0 <= 2 * j < near1:
            fine_faces(j)
            for i in (2 * j, 2 * j + 1):
                va[i + 1] = inv0[i] * w0[i]
    sweep(level0, va, vb, 1, 1, near0 + 1)
    sweep(level0, va, vb, 1, near1 - 1, planes0 - 1)

    gather_all(g2, 1).wait_recv()

    f2 = level2[2]

    def unpack(i):
        parts = []
        for j in range(ngy):
            pack = g2[i * ngy + j]
            parts += [even_part(pack, 1), odd_part(pack, 1)]
        f2[i] = jnp.concatenate(parts, axis=0)

    each(nx2, unpack)

    def cycle(l):
        nx, ny = counts[l]
        step = 2**l
        level = level_refs[l]
        (xa, xb, f, inverse) = level[:4]

        def begin(i):
            xa[i + 1] = inverse[i] * f[i]

        each(nx, begin)
        if l == LEVELS:
            for repeat in range(COARSE_SWEEPS - 1):
                sweep(level, xa, xb, step, 0, nx)
                xa, xb = xb, xa
            return xa
        for repeat in range(NU - 1):
            sweep(level, xa, xb, step, 0, nx)
            xa, xb = xb, xa
        f_next = level_refs[l + 1][2]
        size = max(ny // 2, 4)
        if ny // 2 < EDGE:
            f_next[...] = jnp.zeros(f_next.shape, f_next.dtype)

        def restrict(i):
            r = rest_of(level, xa, 2 * i, step) + rest_of(level, xa, 2 * i + 1, step)
            f_next[i, pl.ds(0, size), :] = 0.5 * pair_lanes(pair_rows(r, i % slots), step)

        each(nx // 2, restrict)
        fine = cycle(l + 1)

        def correct(i):
            slot = i % slots
            stretch(fine[i + 1], slot)
            e = temp[slot, pl.ds(0, xa.shape[1]), :]
            xb[2 * i + 1] = xa[2 * i + 1] + e
            xb[2 * i + 2] = xa[2 * i + 2] + e

        each(nx // 2, correct)
        xa, xb = xb, xa
        for repeat in range(NU):
            sweep(level, xa, xb, step, 0, nx)
            xa, xb = xb, xa
        return xa

    found = cycle(2)

    row2 = pl.multiple_of(gy * cy, 8)
    below2 = pl.multiple_of(jnp.maximum(gy * cy - EDGE, 0), 8)
    above2 = pl.multiple_of(jnp.minimum(gy * cy + cy, ny2 - EDGE), 8)
    for t in range(2 * REACH + 1):
        x = gx + t - REACH
        there = (x >= 0) & (x < nx2)
        plane = jnp.clip(x, 0, nx2 - 1) + 1
        e2[t, pl.ds(EDGE, cy), :] = jnp.where(there, found[plane, pl.ds(row2, cy), :], 0.0)
        low = found[plane, pl.ds(below2, EDGE), :]
        high = found[plane, pl.ds(above2, EDGE), :]
        e2[t, pl.ds(0, EDGE), :] = jnp.where(there & (gy > 0), low, 0.0)
        e2[t, pl.ds(EDGE + cy, EDGE), :] = jnp.where(there & (gy < ngy - 1), high, 0.0)

    for t in range(2 * REACH + 1):
        slot = t % slots
        stretch(e2[t], slot)
        e = temp[slot, pl.ds(EDGE, by + 2 * EDGE), :]
        ua[2 * t + 1] = ub[2 * t + 1] + e
        ua[2 * t + 2] = ub[2 * t + 2] + e
    sweep(level1, ua, ub, 2, 2, planes1 - 2)
    sweep(level1, ub, ua, 2, 3, planes1 - 3)

    for j in range(blocks):
        slot = j % slots
        stretch(ua[first_block + j + 1], slot)
        e = temp[slot, pl.ds(EDGE, rows0), :]
        va[2 * j + 1] = vb[2 * j + 1] + e
        va[2 * j + 2] = vb[2 * j + 2] + e
    sweep(level0, va, vb, 1, 2, planes0 - 2)
    sweep(level0, vb, va, 1, 3, planes0 - 3)
    for i in range(lx):
        product = c0[lx + i] * va[lx + i + 1]
        near = neighbours(level0, va, lx + i, 1)
        own = slice(EDGE, EDGE + ly)
        scaled_ref[i] = product[own]
        rest_ref[i] = w0[lx + i, pl.ds(EDGE, ly), :] - product[own] + near[own]

    window_done(phase_window, 0, REACH)
    window_done(near_window, 0, 1, 0)
    window_done(far_window, 1, 1, 1)
    window_done(coarse_window, 0, REACH)
    gather_all(gp, 0).wait_send()
    gather_all(g2, 1).wait_send()


def solution(mesh):
    ngx, ngy = mesh.shape["gx"], mesh.shape["gy"]
    n = ngx * ngy

    def on_device(right_side, phase):
        lx, ly, nz = right_side.shape
        assert lx == 4 and ly % 32 == 0 and NU == 2
        by, cy = ly // 2, ly // 4
        counts = [(lx * ngx >> l, ly * ngy >> l) for l in range(LEVELS + 1)]
        blocks = 2 * REACH + 1

        def level_scratch(planes, rows, padded_source=False):
            shapes = [planes + 2, planes + 2, planes, planes, planes, planes + 1] + [planes] * 4
            if padded_source:
                shapes[2] = 1
            large = planes * rows * nz * 4 >= LARGE
            types = [jnp.float32] * 5 + [jnp.bfloat16 if large else jnp.float32] * 5
            return [pltpu.VMEM((k, rows, nz), dtype) for k, dtype in zip(shapes, types)]

        scratch = [
            pltpu.VMEM((3 * lx, ly + 2 * EDGE, nz), jnp.float32),
            pltpu.VMEM((blocks, by + 2 * EDGE_PHASE, nz), jnp.bfloat16),
            pltpu.VMEM((blocks, by + 2 * EDGE, nz), jnp.float32),
            pltpu.VMEM((n, by, nz), jnp.bfloat16),
            pltpu.VMEM((n, cy // 2, nz), jnp.float32),
            pltpu.VMEM((1, by, nz), jnp.bfloat16),
            pltpu.VMEM((1, by, nz), jnp.float32),
            pltpu.VMEM((1, cy // 2, nz), jnp.float32),
            pltpu.VMEM((8, max(2 * (by + 2 * EDGE), 2 * counts[2][1], 2 * (cy + 2 * EDGE)), nz), jnp.float32),
            pltpu.VMEM((2 * blocks, by + 2 * EDGE, nz), jnp.float32),
            pltpu.VMEM((blocks, cy + 2 * EDGE, nz), jnp.float32),
        ]
        scratch += level_scratch(3 * lx, ly + 2 * EDGE, True)
        scratch += level_scratch(2 * blocks, by + 2 * EDGE)
        for l in range(2, LEVELS + 1):
            scratch += level_scratch(counts[l][0], max(counts[l][1], EDGE))
        scratch += [pltpu.SemaphoreType.DMA((9,))] * 4
        scratch += [pltpu.SemaphoreType.DMA((3 * blocks,))] * 4
        scratch += [pltpu.SemaphoreType.DMA((2,))] * 2
        return pl.pallas_call(
            functools.partial(kernel, ngx, ngy, counts),
            out_shape=[jax.ShapeDtypeStruct(right_side.shape, jnp.float32)] * 2,
            in_specs=[pl.BlockSpec(memory_space=pltpu.VMEM)] * 2,
            out_specs=[pl.BlockSpec(memory_space=pltpu.VMEM)] * 2,
            scratch_shapes=scratch,
            compiler_params=pltpu.CompilerParams(
                collective_id=0, has_side_effects=True, vmem_limit_bytes=66_000_000
            ),
        )(right_side, phase)

    placed = P("gx", "gy", None)
    return jax.shard_map(
        on_device, mesh=mesh, in_specs=(placed, placed), out_specs=(placed, placed), check_vma=False
    )
```
